32 devices in a mesh: section: 2 (over core), stream: 4 (over y, x), slab: 4 (over z).
Axes of the slice: x: 2, y: 2, z: 4, core: 2. Of those that a mesh axis runs over, the one named last changes fastest.
Arguments:
- state: float32 [2, 4, 256, 64, 128], P('section', None, 'stream', 'slab'), may hold values from -6 to 6
- source_mask: int32 [16, 4], P(None, 'slab'), may hold values 0 or 1
- deriv_x: float32 [256, 256], replicated, may hold values from -0.28125 to 0.28125
- deriv_z: float32 [128, 128], replicated, may hold values from -0.397747564 to 0.397747564
- filter_x: float32 [256, 256], replicated, may hold values from -0.375 to 0.375
- filter_z: float32 [128, 128], replicated, may hold values from -0.5 to 0.5
Outputs:
- advanced: float32 [2, 4, 256, 64, 128], P('section', None, 'stream', 'slab')
The draws below stay inside these ranges and needn't reach their ends.
All inputs are finite; a program needn't handle non-finite values. No bound on the sum of `source_mask` on one device may be relied on, other than what follows from the above.
Results may differ from the reference program's by a relative error of at most 0.0001.
Values sent between devices are 32-bit elements; how exact they have to be, the bound alone decides.
A program may use at most 128 MiB of HBM per device.

```python
import math
import jax
import jax.numpy as jnp
from jax import lax

NX = 256
NZ = 128
SEGMENTS = 8
MBLK = 16
NY = 64


def dense_operator(key, order):
    limit = 4.5 / math.sqrt(order)
    values = jnp.clip(3.0 / math.sqrt(order) * jax.random.normal(key, (order, order), jnp.float32), -limit, limit)
    return values


def draw_deriv_x(key, part):
    return dense_operator(jax.random.fold_in(key, 11), NX)


def draw_deriv_z(key, part):
    return dense_operator(jax.random.fold_in(key, 23), NZ)


def touch_ends(array, stream_key, low, largest):
    dims = array.shape
    place = [jax.random.randint(jax.random.fold_in(stream_key, axis), (), 0, dims[axis]) for axis in range(len(dims))]
    array = array.at[tuple(place)].set(low)
    longest = dims.index(max(dims))
    place[longest] = (place[longest] + 1) % dims[longest]
    return array.at[tuple(place)].set(largest)


def shard_levels(own_key, dims, cuts, least, largest):
    def one(position, blocks):
        steps = jax.random.uniform(jax.random.fold_in(jax.random.fold_in(own_key, 6), position), (blocks,), jnp.float32, least / len(cuts), largest / len(cuts))
        return jnp.repeat(jnp.exp(steps), dims[position] // blocks).reshape((-1,) + (1,) * (len(dims) - position - 1))

    level = one(*cuts[0])
    for cut in cuts[1:]:
        level = level * one(*cut)
    return level


def normal_values(own_key, dims, width, bound, cuts=(), held_as=jnp.bfloat16):
    entries = width * jax.random.normal(own_key, dims, jnp.float32)
    if cuts:
        entries = entries * shard_levels(own_key, dims, cuts, -0.22, 0.18)
    return jnp.clip(entries, -bound, bound).astype(held_as)


def setup_inputs(seed: int = 0) -> dict:
    arg_keys = jax.random.split(jax.random.key(seed), 7)
    return {
        "state": normal_values(arg_keys[0], (2, 4, NX, NY, NZ), 1.0, 6.0, ((0, 2), (2, 4), (3, 4)), jnp.float32),
        "source_mask": touch_ends((jax.random.randint(arg_keys[1], (NX // MBLK, NY // MBLK), 0, 2) < 1).astype(jnp.int32), jax.random.fold_in(arg_keys[1], 1), 0, 1),
        "deriv_x": draw_deriv_x(jax.random.fold_in(arg_keys[6], 71), 0),
        "deriv_z": draw_deriv_z(jax.random.fold_in(arg_keys[6], 71), 0),
        "filter_x": normal_values(arg_keys[4], (NX, NX), NX ** -0.5, 0.375, (), jnp.float32),
        "filter_z": normal_values(arg_keys[5], (NZ, NZ), NZ ** -0.5, 0.5, (), jnp.float32),
    }


mach_number = 0.5
time_step = 0.05
filter_weight = 0.25


def central_slope(values, which_dim):
    widths = [(0, 0), (0, 0), (0, 0)]
    widths[which_dim] = (1, 1)
    padded = jnp.pad(values, widths)
    length = values.shape[which_dim]
    upper_side = lax.slice_in_dim(padded, 2, length + 2, axis=which_dim)
    lower_side = lax.slice_in_dim(padded, 0, length, axis=which_dim)
    return 0.5 * (upper_side - lower_side)


def lamb_vector(velocity):
    speed_x, speed_y, speed_z = velocity[0], velocity[1], velocity[2]
    vortex_x = central_slope(speed_z, 1) - central_slope(speed_y, 2)
    vortex_y = central_slope(speed_x, 2) - central_slope(speed_z, 0)
    vortex_z = central_slope(speed_y, 0) - central_slope(speed_x, 1)
    return jnp.stack([vortex_y * speed_z - vortex_z * speed_y,
                      vortex_z * speed_x - vortex_x * speed_z,
                      vortex_x * speed_y - vortex_y * speed_x])


def along_x(matrix, fields):
    return jnp.einsum("ij,fjyz->fiyz", matrix, fields, precision=lax.Precision.HIGHEST)


def along_z(matrix, fields):
    return jnp.einsum("fxyz,kz->fxyk", fields, matrix, precision=lax.Precision.HIGHEST)


def fourth_slope_y(fields):
    padded = jnp.pad(fields, ((0, 0), (0, 0), (2, 2), (0, 0)))
    length = fields.shape[2]

    def shifted(offset):
        return lax.slice_in_dim(padded, 2 + offset, 2 + offset + length, axis=2)

    return (8.0 * (shifted(1) - shifted(-1)) - (shifted(2) - shifted(-2))) / 12.0


def tendency(fields, slope_x, slope_y, slope_z, forcing):
    press_rate = -mach_number * slope_x[0] - slope_x[1] - slope_y[1] - slope_z[1]
    axial_rate = -mach_number * slope_x[1] - slope_x[0] + forcing[0]
    normal_rate = -mach_number * slope_x[2] - slope_y[0] + forcing[1]
    third_rate = -mach_number * slope_x[3] - slope_z[0] + forcing[2]
    return jnp.stack([press_rate, axial_rate, normal_rate, third_rate])


def substep(fields, forcing, deriv_x, deriv_z):
    slope_x = along_x(deriv_x, fields)
    slope_y = fourth_slope_y(jnp.stack([fields[0], fields[2]]))
    slope_z = along_z(deriv_z, jnp.stack([fields[0], fields[3]]))
    return fields + time_step * tendency(fields, slope_x, slope_y, slope_z, forcing)


def reference(state, source_mask, deriv_x, deriv_z, filter_x, filter_z):
    region = jnp.repeat(jnp.repeat(source_mask, MBLK, axis=0), MBLK, axis=1).astype(jnp.float32)
    flow_now = state[0]
    sound_now = state[1]
    no_forcing = jnp.zeros((3,) + flow_now.shape[1:], jnp.float32)
    forcing = no_forcing
    for segment_index in range(SEGMENTS):
        if segment_index % 2 == 0:
            forcing = -region[None, :, :, None] * lamb_vector(flow_now[1:4])
        flow_now = substep(flow_now, no_forcing, deriv_x, deriv_z)
        sound_now = substep(sound_now, forcing, deriv_x, deriv_z)

    def smooth(fields):
        return fields + filter_weight * along_x(filter_x, fields) + filter_weight * along_z(filter_z, fields)

    return jnp.stack([smooth(flow_now), smooth(sound_now)])
```

```python
import functools
import math

import jax
import jax.numpy as jnp
from jax import lax
from jax.experimental import pallas as pl
from jax.experimental.pallas import tpu as pltpu
from jax.sharding import PartitionSpec as P

SEGMENTS = 8
MBLK = 16

mach_number = 0.5
time_step = 0.05
filter_weight = 0.25


def split_parts(value):
    high = value.astype(jnp.bfloat16)
    low = (value - high.astype(jnp.float32)).astype(jnp.bfloat16)
    return high, low


def dot_parts(left, right):
    dot = functools.partial(jnp.dot, preferred_element_type=jnp.float32)
    return dot(left[0], right[0]) + (dot(left[0], right[1]) + dot(left[1], right[0]))


def wide(ref):
    return jnp.concatenate([ref[0, i] for i in range(4)], axis=1)


def local_kernel(fields_ref, dx_ref, dzt_ref, out_ref):
    nz = fields_ref.shape[3]
    nx = fields_ref.shape[2]
    dx = split_parts(dx_ref[...])
    dzt = split_parts(dzt_ref[...])
    fields = wide(fields_ref)
    sx = dot_parts(dx, split_parts(fields))
    sz = dot_parts(split_parts(jnp.concatenate([fields_ref[0, 0], fields_ref[0, 3]], axis=0)), dzt)
    sp, su, sv, sw = (sx[:, i * nz:(i + 1) * nz] for i in range(4))
    out_ref[0, 0] = fields_ref[0, 0] - time_step * (mach_number * sp + su + sz[nx:])
    out_ref[0, 1] = fields_ref[0, 1] - time_step * (mach_number * su + sp)
    out_ref[0, 2] = fields_ref[0, 2] - (time_step * mach_number) * sv
    out_ref[0, 3] = fields_ref[0, 3] - time_step * (mach_number * sw + sz[:nx])


def filter_kernel(fields_ref, fx_ref, fzt_ref, out_ref):
    nz = fields_ref.shape[3]
    nx = fields_ref.shape[2]
    fx = split_parts(fx_ref[...])
    fzt = split_parts(fzt_ref[...])
    sx = dot_parts(fx, split_parts(wide(fields_ref)))
    sz = dot_parts(split_parts(jnp.concatenate([fields_ref[0, i] for i in range(4)], axis=0)), fzt)
    for i in range(4):
        out_ref[0, i] = fields_ref[0, i] + filter_weight * (sx[:, i * nz:(i + 1) * nz] + sz[i * nx:(i + 1) * nx])


def row_call(kernel, fields, mat_x, mat_zt):
    rows, count, nx, nz = fields.shape
    block = pl.BlockSpec((1, count, nx, nz), lambda i: (i, 0, 0, 0))
    return pl.pallas_call(
        kernel,
        grid=(rows,),
        in_specs=[block, pl.BlockSpec((nx, nx), lambda i: (0, 0)), pl.BlockSpec((nz, nz), lambda i: (0, 0))],
        out_specs=block,
        out_shape=jax.ShapeDtypeStruct(fields.shape, jnp.float32),
        cost_estimate=pl.CostEstimate(
            flops=6 * rows * count * nx * nz * (nx + nz), bytes_accessed=8 * fields.size, transcendentals=0
        ),
    )(fields, mat_x, mat_zt)


def chain(streams, slabs):
    side = math.isqrt(streams)
    path = list(range(streams))
    if side * side == streams:
        path = [r * side + (c if r % 2 == 0 else side - 1 - c) for r in range(side) for c in range(side)]
    place = [path.index(s) for s in range(streams)]
    order = []
    for k in range(slabs):
        order += [s * slabs + k for s in (path if k % 2 == 0 else path[::-1])]
    return place, order


def neighbour_rows(values, width, order, sections):
    rows = values.shape[0]
    total = len(order)
    axes = ("section", "stream", "slab")

    def shift(part, steps):
        pairs = []
        for section in range(sections):
            for g in range(total):
                if 0 <= g + steps < total:
                    pairs.append((section * total + order[g], section * total + order[g + steps]))
        return lax.ppermute(part, axes, pairs)

    if rows >= width:
        return shift(values[rows - width:], 1), shift(values[:width], -1)
    reach = -(-width // rows)
    before = jnp.concatenate([shift(values, d) for d in range(reach, 0, -1)], axis=0)
    after = jnp.concatenate([shift(values, -d) for d in range(1, reach + 1)], axis=0)
    return before[reach * rows - width:], after[:width]


def slope(values, dim):
    pads = [(0, 0)] * values.ndim
    pads[dim] = (1, 1)
    padded = jnp.pad(values, pads)
    length = values.shape[dim]
    return 0.5 * (
        lax.slice_in_dim(padded, 2, length + 2, axis=dim) - lax.slice_in_dim(padded, 0, length, axis=dim)
    )


def lamb(fields, before, after):
    u, v, w = fields[:, 1], fields[:, 2], fields[:, 3]
    rows = fields.shape[0]
    near = jnp.concatenate([before, jnp.stack([u, w], axis=1), after], axis=0)
    c2 = 0.5 * (near[2:] - near[:rows])
    ox = c2[:, 1] - slope(v, 2)
    oy = slope(u, 2) - slope(w, 1)
    oz = slope(v, 1) - c2[:, 0]
    return jnp.stack([oy * w - oz * v, oz * u - ox * w, ox * v - oy * u], axis=1)


def shards(state, source_mask, deriv_x, deriv_z, filter_x, filter_z):
    streams, slabs = lax.axis_size("stream"), lax.axis_size("slab")
    place, order = chain(streams, slabs)
    fields = state[0]
    count, width_x, width_y, nz = fields.shape
    nx = width_x * streams
    rows = width_y // streams
    even = lax.axis_index("slab") % 2 == 0
    back = [streams - 1 - p for p in place]

    parts = fields.reshape(count, width_x, streams, rows, nz).transpose(2, 3, 0, 1, 4)
    parts = jnp.where(even, jnp.stack([parts[p] for p in place]), jnp.stack([parts[p] for p in back]))
    parts = lax.all_to_all(parts, "stream", split_axis=0, concat_axis=0, tiled=True)
    fields = parts.transpose(1, 2, 0, 3, 4).reshape(rows, count, nx, nz)

    blocks = source_mask.astype(jnp.float32)
    region = jnp.repeat(jnp.repeat(blocks, MBLK, axis=0), MBLK, axis=1).T
    mine = jnp.asarray(place)[lax.axis_index("stream")]
    mine = jnp.where(even, mine, streams - 1 - mine)
    region = lax.dynamic_slice_in_dim(region, mine * rows, rows, 0)[:, None, :, None]
    deriv_zt, filter_zt = deriv_z.T, filter_z.T

    forcing = None
    for segment in range(SEGMENTS):
        pv = jnp.stack([fields[:, 0], fields[:, 2]], axis=1)
        before, after = neighbour_rows(pv, 2, order, 2)
        if segment % 2 == 0:
            uw = jnp.stack([fields[:, 1], fields[:, 3]], axis=1)
            low, high = neighbour_rows(uw, 1, order, 1)
            source = -region * lamb(fields, low, high)
            forcing = lax.ppermute(source, "section", [(0, 1)])
        part = row_call(local_kernel, fields, deriv_x, deriv_zt)
        near = jnp.concatenate([before, pv, after], axis=0)
        dy = (8.0 * (near[3:3 + rows] - near[1:1 + rows]) - (near[4:4 + rows] - near[:rows])) / 12.0
        fields = jnp.stack(
            [
                part[:, 0] - time_step * dy[:, 1],
                part[:, 1] + time_step * forcing[:, 0],
                part[:, 2] + time_step * (forcing[:, 1] - dy[:, 0]),
                part[:, 3] + time_step * forcing[:, 2],
            ],
            axis=1,
        )
    fields = row_call(filter_kernel, fields, filter_x, filter_zt)

    parts = fields.reshape(rows, count, streams, width_x, nz).transpose(2, 0, 1, 3, 4)
    parts = lax.all_to_all(parts, "stream", split_axis=0, concat_axis=0, tiled=True)
    inv_place = [place.index(j) for j in range(streams)]
    inv_back = [back.index(j) for j in range(streams)]
    parts = jnp.where(even, jnp.stack([parts[p] for p in inv_place]), jnp.stack([parts[p] for p in inv_back]))
    return parts.transpose(2, 3, 0, 1, 4).reshape(1, count, width_x, width_y, nz)


def solution(mesh):
    placed = (P("section", None, "stream", "slab", None), P(None, "slab"), P(), P(), P(), P())
    return jax.shard_map(
        shards,
        mesh=mesh,
        in_specs=placed,
        out_specs=P("section", None, "stream", "slab", None),
        check_vma=False,
    )
```

```python
import functools
import math

import jax
import jax.numpy as jnp
from jax import lax
from jax.experimental import pallas as pl
from jax.experimental.pallas import tpu as pltpu
from jax.sharding import PartitionSpec as P

SEGMENTS = 8
MBLK = 16

mach_number = 0.5
time_step = 0.05
filter_weight = 0.25


def split_parts(value):
    high = value.astype(jnp.bfloat16)
    low = (value - high.astype(jnp.float32)).astype(jnp.bfloat16)
    return high, low


def dot_parts(left, right):
    dot = functools.partial(jnp.dot, preferred_element_type=jnp.float32)
    return dot(left[0], right[0]) + (dot(left[0], right[1]) + dot(left[1], right[0]))


def wide(ref):
    return jnp.concatenate([ref[0, i] for i in range(4)], axis=1)


def local_kernel(fields_ref, dx_ref, dzt_ref, out_ref):
    nz = fields_ref.shape[3]
    nx = fields_ref.shape[2]
    dx = split_parts(dx_ref[...])
    dzt = split_parts(dzt_ref[...])
    fields = wide(fields_ref)
    sx = dot_parts(dx, split_parts(fields))
    sz = dot_parts(split_parts(jnp.concatenate([fields_ref[0, 0], fields_ref[0, 3]], axis=0)), dzt)
    sp, su, sv, sw = (sx[:, i * nz:(i + 1) * nz] for i in range(4))
    out_ref[0, 0] = fields_ref[0, 0] - time_step * (mach_number * sp + su + sz[nx:])
    out_ref[0, 1] = fields_ref[0, 1] - time_step * (mach_number * su + sp)
    out_ref[0, 2] = fields_ref[0, 2] - (time_step * mach_number) * sv
    out_ref[0, 3] = fields_ref[0, 3] - time_step * (mach_number * sw + sz[:nx])


def filter_kernel(fields_ref, fx_ref, fzt_ref, out_ref):
    nz = fields_ref.shape[3]
    nx = fields_ref.shape[2]
    fx = split_parts(fx_ref[...])
    fzt = split_parts(fzt_ref[...])
    sx = dot_parts(fx, split_parts(wide(fields_ref)))
    sz = dot_parts(split_parts(jnp.concatenate([fields_ref[0, i] for i in range(4)], axis=0)), fzt)
    for i in range(4):
        out_ref[0, i] = fields_ref[0, i] + filter_weight * (sx[:, i * nz:(i + 1) * nz] + sz[i * nx:(i + 1) * nx])


def row_call(kernel, fields, mat_x, mat_zt):
    rows, count, nx, nz = fields.shape
    block = pl.BlockSpec((1, count, nx, nz), lambda i: (i, 0, 0, 0))
    return pl.pallas_call(
        kernel,
        grid=(rows,),
        in_specs=[block, pl.BlockSpec((nx, nx), lambda i: (0, 0)), pl.BlockSpec((nz, nz), lambda i: (0, 0))],
        out_specs=block,
        out_shape=jax.ShapeDtypeStruct(fields.shape, jnp.float32),
        cost_estimate=pl.CostEstimate(
            flops=6 * rows * count * nx * nz * (nx + nz), bytes_accessed=8 * fields.size, transcendentals=0
        ),
    )(fields, mat_x, mat_zt)


def chain(streams, slabs):
    side = math.isqrt(streams)
    path = list(range(streams))
    if side * side == streams:
        path = [r * side + (c if r % 2 == 0 else side - 1 - c) for r in range(side) for c in range(side)]
    place = [path.index(s) for s in range(streams)]
    order = []
    for k in range(slabs):
        order += [s * slabs + k for s in (path if k % 2 == 0 else path[::-1])]
    return place, order


def neighbour_rows(values, width, order, sections):
    rows = values.shape[0]
    total = len(order)
    axes = ("section", "stream", "slab")

    def shift(part, steps):
        pairs = []
        for section in range(sections):
            for g in range(total):
                if 0 <= g + steps < total:
                    pairs.append((section * total + order[g], section * total + order[g + steps]))
        return lax.ppermute(part, axes, pairs)

    if rows >= width:
        return shift(values[rows - width:], 1), shift(values[:width], -1)
    reach = -(-width // rows)
    before = jnp.concatenate([shift(values, d) for d in range(reach, 0, -1)], axis=0)
    after = jnp.concatenate([shift(values, -d) for d in range(1, reach + 1)], axis=0)
    return before[reach * rows - width:], after[:width]


def slope(values, dim):
    pads = [(0, 0)] * values.ndim
    pads[dim] = (1, 1)
    padded = jnp.pad(values, pads)
    length = values.shape[dim]
    return 0.5 * (
        lax.slice_in_dim(padded, 2, length + 2, axis=dim) - lax.slice_in_dim(padded, 0, length, axis=dim)
    )


def lamb(fields, before, after):
    u, v, w = fields[:, 1], fields[:, 2], fields[:, 3]
    rows = fields.shape[0]
    near = jnp.concatenate([before, jnp.stack([u, w], axis=1), after], axis=0)
    c2 = 0.5 * (near[2:] - near[:rows])
    ox = c2[:, 1] - slope(v, 2)
    oy = slope(u, 2) - slope(w, 1)
    oz = slope(v, 1) - c2[:, 0]
    return jnp.stack([oy * w - oz * v, oz * u - ox * w, ox * v - oy * u], axis=1)


def shift_masked(value, dim, step):
    size = value.shape[dim]
    moved = pltpu.roll(value, (-step) % size, dim)
    index = lax.broadcasted_iota(jnp.int32, value.shape, dim)
    return jnp.where(index == (size - 1 if step > 0 else 0), 0.0, moved)


def inner_slope(value, dim):
    return 0.5 * (shift_masked(value, dim, 1) - shift_masked(value, dim, -1))


def fold(index, side):
    row = index // side
    col = index % side
    return row * side + col + (row % 2) * (side - 1 - 2 * col)


def steps_kernel(streams, slabs, pv_ref, uw_ref, region_ref, dx_ref, dzt_ref, fx_ref, fzt_ref, out_ref,
                 pv, uw, part, source, forcing, dxs, dzs, pv_send, pv_recv, uw_send, uw_recv, src_send, src_recv, credit):
    rows, _, nx, nz = pv_ref.shape
    total = streams * slabs
    side = math.isqrt(streams)
    side = side if side * side == streams else streams
    section, stream, slab = lax.axis_index("section"), lax.axis_index("stream"), lax.axis_index("slab")

    def turn(place, which):
        return place + (which % 2) * (streams - 1 - 2 * place)

    def device_at(spot):
        which = spot // streams
        return (section, fold(turn(spot % streams, which), side), which)

    spot = slab * streams + turn(fold(stream, side), slab)
    has_low, has_high = spot > 0, spot < total - 1
    low = device_at(jnp.maximum(spot - 1, 0))
    high = device_at(jnp.minimum(spot + 1, total - 1))
    partner = (1 - section, stream, slab)
    is_flow, is_sound = section == 0, section == 1

    def remote(src, dst, send, recv, device):
        return pltpu.make_async_remote_copy(
            src_ref=src, dst_ref=dst, send_sem=send, recv_sem=recv,
            device_id=device, device_id_type=pl.DeviceIdType.MESH,
        )

    def pv_up(slot):
        return remote(pv.at[slot, pl.ds(rows, 2)], pv.at[slot, pl.ds(0, 2)], pv_send.at[slot, 0], pv_recv.at[slot, 0], high)

    def pv_down(slot):
        return remote(pv.at[slot, pl.ds(2, 2)], pv.at[slot, pl.ds(rows + 2, 2)], pv_send.at[slot, 1], pv_recv.at[slot, 1], low)

    def uw_up():
        return remote(uw.at[rows], uw.at[0], uw_send.at[0], uw_recv.at[0], high)

    def uw_down():
        return remote(uw.at[1], uw.at[rows + 1], uw_send.at[1], uw_recv.at[1], low)

    def src_copy():
        return remote(source, forcing, src_send, src_recv, partner)

    def start_both(up, down):
        @pl.when(has_high)
        def _():
            up.start()

        @pl.when(has_low)
        def _():
            down.start()

    def wait_both(up, down):
        @pl.when(has_low)
        def _():
            up.wait_recv()
            down.wait_send()

        @pl.when(has_high)
        def _():
            down.wait_recv()
            up.wait_send()

    def start_uw():
        @pl.when(is_flow)
        def _():
            start_both(uw_up(), uw_down())

    def each_row(body):
        def step(row, carry):
            body(row)
            return carry

        lax.fori_loop(0, rows, step, 0)

    for slot in range(2):
        for edge in range(2):
            pv[slot, edge] = jnp.zeros((2, nx, nz), jnp.float32)
            pv[slot, rows + 2 + edge] = jnp.zeros((2, nx, nz), jnp.float32)
    uw[0] = jnp.zeros((2, nx, nz), jnp.float32)
    uw[rows + 1] = jnp.zeros((2, nx, nz), jnp.float32)

    def load(row):
        pv[0, row + 2] = pv_ref[row]
        uw[row + 1] = uw_ref[row]

    each_row(load)

    barrier = pltpu.get_barrier_semaphore()

    def greet(device):
        pl.semaphore_signal(barrier, inc=1, device_id=device, device_id_type=pl.DeviceIdType.MESH)

    greet(partner)

    @pl.when(has_low)
    def _():
        greet(low)

    @pl.when(has_high)
    def _():
        greet(high)

    pl.semaphore_wait(barrier, 1 + has_low.astype(jnp.int32) + has_high.astype(jnp.int32))

    def put_matrix(mat_x, mat_z):
        dxs[0], dxs[1] = split_parts(mat_x[...])
        dzs[0], dzs[1] = split_parts(mat_z[...])

    def operators(slot):
        def body(row):
            p, v, u, w = pv[slot, row + 2, 0], pv[slot, row + 2, 1], uw[row + 1, 0], uw[row + 1, 1]
            sx = dot_parts((dxs[0], dxs[1]), split_parts(jnp.concatenate([p, u, v, w], axis=1)))
            sz = dot_parts(split_parts(jnp.concatenate([p, w], axis=0)), (dzs[0], dzs[1]))
            sp, su, sv, sw = (sx[:, i * nz:(i + 1) * nz] for i in range(4))
            part[row, 0] = p - time_step * (mach_number * sp + su + sz[nx:])
            part[row, 1] = u - time_step * (mach_number * su + sp)
            part[row, 2] = v - (time_step * mach_number) * sv
            part[row, 3] = w - time_step * (mach_number * sw + sz[:nx])

        each_row(body)

    def add_forcing():
        def body(row):
            for i in range(3):
                part[row, i + 1] = part[row, i + 1] + time_step * forcing[row, i]

        each_row(body)

    def keep_uw():
        def body(row):
            uw[row + 1, 0] = part[row, 1]
            uw[row + 1, 1] = part[row, 3]

        each_row(body)

    def update_pv(slot):
        def body(row):
            def dy(field):
                ahead = pv[slot, row + 3, field] - pv[slot, row + 1, field]
                return (8.0 * ahead - (pv[slot, row + 4, field] - pv[slot, row, field])) / 12.0

            pv[1 - slot, row + 2, 0] = part[row, 0] - time_step * dy(1)
            pv[1 - slot, row + 2, 1] = part[row, 2] - time_step * dy(0)

        each_row(body)

    def lamb_rows():
        def body(row):
            u, v, w = uw[row + 1, 0], pv[0, row + 2, 1], uw[row + 1, 1]
            ox = 0.5 * (uw[row + 2, 1] - uw[row, 1]) - inner_slope(v, 1)
            oy = inner_slope(u, 1) - inner_slope(w, 0)
            oz = inner_slope(v, 0) - 0.5 * (uw[row + 2, 0] - uw[row, 0])
            mask = -region_ref[row]
            source[row, 0] = mask * (oy * w - oz * v)
            source[row, 1] = mask * (oz * u - ox * w)
            source[row, 2] = mask * (ox * v - oy * u)

        each_row(body)

    put_matrix(dx_ref, dzt_ref)
    start_uw()
    start_both(pv_up(0), pv_down(0))
    pairs = SEGMENTS // 2

    def pair(m, carry):
        operators(0)

        @pl.when(is_flow)
        def _():
            wait_both(uw_up(), uw_down())
            lamb_rows()

            @pl.when(m > 0)
            def _():
                pl.semaphore_wait(credit, 1)

            src_copy().start()

        @pl.when(is_sound)
        def _():
            src_copy().wait_recv()
            add_forcing()

        wait_both(pv_up(0), pv_down(0))
        update_pv(0)
        start_both(pv_up(1), pv_down(1))
        keep_uw()
        operators(1)

        @pl.when(is_sound)
        def _():
            add_forcing()

            @pl.when(m < pairs - 1)
            def _():
                pl.semaphore_signal(credit, inc=1, device_id=partner, device_id_type=pl.DeviceIdType.MESH)

        @pl.when(is_flow)
        def _():
            src_copy().wait_send()

        keep_uw()
        wait_both(pv_up(1), pv_down(1))

        @pl.when(m < pairs - 1)
        def _():
            start_uw()

        update_pv(1)

        @pl.when(m < pairs - 1)
        def _():
            start_both(pv_up(0), pv_down(0))

        return carry

    lax.fori_loop(0, pairs, pair, 0)

    put_matrix(fx_ref, fzt_ref)

    def smooth(row):
        group = (pv[0, row + 2, 0], uw[row + 1, 0], pv[0, row + 2, 1], uw[row + 1, 1])
        sx = dot_parts((dxs[0], dxs[1]), split_parts(jnp.concatenate(group, axis=1)))
        sz = dot_parts(split_parts(jnp.concatenate(group, axis=0)), (dzs[0], dzs[1]))
        for i in range(4):
            out_ref[row, i] = group[i] + filter_weight * (sx[:, i * nz:(i + 1) * nz] + sz[i * nx:(i + 1) * nx])

    each_row(smooth)


def steps_call(streams, slabs, fields, region, deriv_x, deriv_zt, filter_x, filter_zt):
    rows, count, nx, nz = fields.shape
    pv = jnp.stack([fields[:, 0], fields[:, 2]], axis=1)
    uw = jnp.stack([fields[:, 1], fields[:, 3]], axis=1)
    f32 = jnp.float32
    dma = pltpu.SemaphoreType.DMA
    return pl.pallas_call(
        functools.partial(steps_kernel, streams, slabs),
        out_shape=jax.ShapeDtypeStruct(fields.shape, f32),
        in_specs=[pl.BlockSpec(memory_space=pltpu.VMEM)] * 7,
        out_specs=pl.BlockSpec(memory_space=pltpu.VMEM),
        scratch_shapes=[
            pltpu.VMEM((2, rows + 4, 2, nx, nz), f32),
            pltpu.VMEM((rows + 2, 2, nx, nz), f32),
            pltpu.VMEM((rows, 4, nx, nz), f32),
            pltpu.VMEM((rows, 3, nx, nz), f32),
            pltpu.VMEM((rows, 3, nx, nz), f32),
            pltpu.VMEM((2, nx, nx), jnp.bfloat16),
            pltpu.VMEM((2, nz, nz), jnp.bfloat16),
            dma((2, 2)), dma((2, 2)), dma((2,)), dma((2,)), dma, dma,
            pltpu.SemaphoreType.REGULAR,
        ],
        compiler_params=pltpu.CompilerParams(
            collective_id=0, has_side_effects=True, vmem_limit_bytes=48 * 1024 * 1024
        ),
    )(pv, uw, jnp.broadcast_to(region, (rows, nx, nz)), deriv_x, deriv_zt, filter_x, filter_zt)


def plain_steps(order, fields, region, deriv_x, deriv_zt, filter_x, filter_zt):
    rows = fields.shape[0]
    forcing = None
    for segment in range(SEGMENTS):
        pv = jnp.stack([fields[:, 0], fields[:, 2]], axis=1)
        before, after = neighbour_rows(pv, 2, order, 2)
        if segment % 2 == 0:
            uw = jnp.stack([fields[:, 1], fields[:, 3]], axis=1)
            low, high = neighbour_rows(uw, 1, order, 1)
            source = -region * lamb(fields, low, high)
            forcing = lax.ppermute(source, "section", [(0, 1)])
        part = row_call(local_kernel, fields, deriv_x, deriv_zt)
        near = jnp.concatenate([before, pv, after], axis=0)
        dy = (8.0 * (near[3:3 + rows] - near[1:1 + rows]) - (near[4:4 + rows] - near[:rows])) / 12.0
        fields = jnp.stack(
            [
                part[:, 0] - time_step * dy[:, 1],
                part[:, 1] + time_step * forcing[:, 0],
                part[:, 2] + time_step * (forcing[:, 1] - dy[:, 0]),
                part[:, 3] + time_step * forcing[:, 2],
            ],
            axis=1,
        )
    return row_call(filter_kernel, fields, filter_x, filter_zt)


def shards(state, source_mask, deriv_x, deriv_z, filter_x, filter_z):
    streams, slabs = lax.axis_size("stream"), lax.axis_size("slab")
    place, order = chain(streams, slabs)
    fields = state[0]
    count, width_x, width_y, nz = fields.shape
    nx = width_x * streams
    rows = width_y // streams
    even = lax.axis_index("slab") % 2 == 0
    back = [streams - 1 - p for p in place]

    parts = fields.reshape(count, width_x, streams, rows, nz).transpose(2, 3, 0, 1, 4)
    parts = jnp.where(even, jnp.stack([parts[p] for p in place]), jnp.stack([parts[p] for p in back]))
    parts = lax.all_to_all(parts, "stream", split_axis=0, concat_axis=0, tiled=True)
    fields = parts.transpose(1, 2, 0, 3, 4).reshape(rows, count, nx, nz)

    blocks = source_mask.astype(jnp.float32)
    region = jnp.repeat(jnp.repeat(blocks, MBLK, axis=0), MBLK, axis=1).T
    mine = jnp.asarray(place)[lax.axis_index("stream")]
    mine = jnp.where(even, mine, streams - 1 - mine)
    region = lax.dynamic_slice_in_dim(region, mine * rows, rows, 0)[:, None, :, None]
    deriv_zt, filter_zt = deriv_z.T, filter_z.T

    mats = (deriv_x, deriv_zt, filter_x, filter_zt)
    if rows >= 2:
        fields = steps_call(streams, slabs, fields, region[:, 0], *mats)
    else:
        fields = plain_steps(order, fields, region, *mats)

    parts = fields.reshape(rows, count, streams, width_x, nz).transpose(2, 0, 1, 3, 4)
    parts = lax.all_to_all(parts, "stream", split_axis=0, concat_axis=0, tiled=True)
    inv_place = [place.index(j) for j in range(streams)]
    inv_back = [back.index(j) for j in range(streams)]
    parts = jnp.where(even, jnp.stack([parts[p] for p in inv_place]), jnp.stack([parts[p] for p in inv_back]))
    return parts.transpose(2, 3, 0, 1, 4).reshape(1, count, width_x, width_y, nz)


def solution(mesh):
    placed = (P("section", None, "stream", "slab", None), P(None, "slab"), P(), P(), P(), P())
    return jax.shard_map(
        shards,
        mesh=mesh,
        in_specs=placed,
        out_specs=P("section", None, "stream", "slab", None),
        check_vma=False,
    )
```

```python
import functools
import math

import jax
import jax.numpy as jnp
from jax import lax
from jax.experimental import pallas as pl
from jax.experimental.pallas import tpu as pltpu
from jax.sharding import PartitionSpec as P

SEGMENTS = 8
MBLK = 16

mach_number = 0.5
time_step = 0.05
filter_weight = 0.25


def split_parts(value):
    high = value.astype(jnp.bfloat16)
    low = (value - high.astype(jnp.float32)).astype(jnp.bfloat16)
    return high, low


def dot_parts(left, right):
    dot = functools.partial(jnp.dot, preferred_element_type=jnp.float32)
    return dot(left[0], right[0]) + (dot(left[0], right[1]) + dot(left[1], right[0]))


def wide(ref):
    return jnp.concatenate([ref[0, i] for i in range(4)], axis=1)


def local_kernel(fields_ref, dx_ref, dzt_ref, out_ref):
    nz = fields_ref.shape[3]
    nx = fields_ref.shape[2]
    dx = split_parts(dx_ref[...])
    dzt = split_parts(dzt_ref[...])
    fields = wide(fields_ref)
    sx = dot_parts(dx, split_parts(fields))
    sz = dot_parts(split_parts(jnp.concatenate([fields_ref[0, 0], fields_ref[0, 3]], axis=0)), dzt)
    sp, su, sv, sw = (sx[:, i * nz:(i + 1) * nz] for i in range(4))
    out_ref[0, 0] = fields_ref[0, 0] - time_step * (mach_number * sp + su + sz[nx:])
    out_ref[0, 1] = fields_ref[0, 1] - time_step * (mach_number * su + sp)
    out_ref[0, 2] = fields_ref[0, 2] - (time_step * mach_number) * sv
    out_ref[0, 3] = fields_ref[0, 3] - time_step * (mach_number * sw + sz[:nx])


def filter_kernel(fields_ref, fx_ref, fzt_ref, out_ref):
    nz = fields_ref.shape[3]
    nx = fields_ref.shape[2]
    fx = split_parts(fx_ref[...])
    fzt = split_parts(fzt_ref[...])
    sx = dot_parts(fx, split_parts(wide(fields_ref)))
    sz = dot_parts(split_parts(jnp.concatenate([fields_ref[0, i] for i in range(4)], axis=0)), fzt)
    for i in range(4):
        out_ref[0, i] = fields_ref[0, i] + filter_weight * (sx[:, i * nz:(i + 1) * nz] + sz[i * nx:(i + 1) * nx])


def row_call(kernel, fields, mat_x, mat_zt):
    rows, count, nx, nz = fields.shape
    block = pl.BlockSpec((1, count, nx, nz), lambda i: (i, 0, 0, 0))
    return pl.pallas_call(
        kernel,
        grid=(rows,),
        in_specs=[block, pl.BlockSpec((nx, nx), lambda i: (0, 0)), pl.BlockSpec((nz, nz), lambda i: (0, 0))],
        out_specs=block,
        out_shape=jax.ShapeDtypeStruct(fields.shape, jnp.float32),
        cost_estimate=pl.CostEstimate(
            flops=6 * rows * count * nx * nz * (nx + nz), bytes_accessed=8 * fields.size, transcendentals=0
        ),
    )(fields, mat_x, mat_zt)


def chain(streams, slabs):
    side = math.isqrt(streams)
    path = list(range(streams))
    if side * side == streams:
        path = [r * side + (c if r % 2 == 0 else side - 1 - c) for r in range(side) for c in range(side)]
    place = [path.index(s) for s in range(streams)]
    order = []
    for k in range(slabs):
        order += [s * slabs + k for s in (path if k % 2 == 0 else path[::-1])]
    return place, order


def neighbour_rows(values, width, order, sections):
    rows = values.shape[0]
    total = len(order)
    axes = ("section", "stream", "slab")

    def shift(part, steps):
        pairs = []
        for section in range(sections):
            for g in range(total):
                if 0 <= g + steps < total:
                    pairs.append((section * total + order[g], section * total + order[g + steps]))
        return lax.ppermute(part, axes, pairs)

    if rows >= width:
        return shift(values[rows - width:], 1), shift(values[:width], -1)
    reach = -(-width // rows)
    before = jnp.concatenate([shift(values, d) for d in range(reach, 0, -1)], axis=0)
    after = jnp.concatenate([shift(values, -d) for d in range(1, reach + 1)], axis=0)
    return before[reach * rows - width:], after[:width]


def slope(values, dim):
    pads = [(0, 0)] * values.ndim
    pads[dim] = (1, 1)
    padded = jnp.pad(values, pads)
    length = values.shape[dim]
    return 0.5 * (
        lax.slice_in_dim(padded, 2, length + 2, axis=dim) - lax.slice_in_dim(padded, 0, length, axis=dim)
    )


def lamb(fields, before, after):
    u, v, w = fields[:, 1], fields[:, 2], fields[:, 3]
    rows = fields.shape[0]
    near = jnp.concatenate([before, jnp.stack([u, w], axis=1), after], axis=0)
    c2 = 0.5 * (near[2:] - near[:rows])
    ox = c2[:, 1] - slope(v, 2)
    oy = slope(u, 2) - slope(w, 1)
    oz = slope(v, 1) - c2[:, 0]
    return jnp.stack([oy * w - oz * v, oz * u - ox * w, ox * v - oy * u], axis=1)


def shift_masked(value, dim, step):
    size = value.shape[dim]
    moved = pltpu.roll(value, (-step) % size, dim)
    index = lax.broadcasted_iota(jnp.int32, value.shape, dim)
    return jnp.where(index == (size - 1 if step > 0 else 0), 0.0, moved)


def inner_slope(value, dim):
    return 0.5 * (shift_masked(value, dim, 1) - shift_masked(value, dim, -1))


def fold(index, side):
    row = index // side
    col = index % side
    return row * side + col + (row % 2) * (side - 1 - 2 * col)


def steps_kernel(streams, slabs, pv_ref, uw_ref, region_ref, dx_ref, dzt_ref, fx_ref, fzt_ref, out_ref,
                 pv, uw, edge, part, source, forcing, dxs, dzs, pv_send, pv_recv, uw_send, uw_recv, src_send, src_recv, credit):
    rows, _, nx, nz = pv_ref.shape
    total = streams * slabs
    side = math.isqrt(streams)
    side = side if side * side == streams else streams
    section, stream, slab = lax.axis_index("section"), lax.axis_index("stream"), lax.axis_index("slab")

    def turn(place, which):
        return place + (which % 2) * (streams - 1 - 2 * place)

    def device_at(spot):
        which = spot // streams
        return (section, fold(turn(spot % streams, which), side), which)

    spot = slab * streams + turn(fold(stream, side), slab)
    has_low, has_high = spot > 0, spot < total - 1
    low = device_at(jnp.maximum(spot - 1, 0))
    high = device_at(jnp.minimum(spot + 1, total - 1))
    partner = (1 - section, stream, slab)
    is_flow, is_sound = section == 0, section == 1

    def remote(src, dst, send, recv, device):
        return pltpu.make_async_remote_copy(
            src_ref=src, dst_ref=dst, send_sem=send, recv_sem=recv,
            device_id=device, device_id_type=pl.DeviceIdType.MESH,
        )

    def pv_up(slot):
        return remote(pv.at[slot, pl.ds(rows, 2)], pv.at[slot, pl.ds(0, 2)], pv_send.at[slot, 0], pv_recv.at[slot, 0], high)

    def pv_down(slot):
        return remote(pv.at[slot, pl.ds(2, 2)], pv.at[slot, pl.ds(rows + 2, 2)], pv_send.at[slot, 1], pv_recv.at[slot, 1], low)

    def uw_up():
        return remote(uw.at[rows], uw.at[0], uw_send.at[0], uw_recv.at[0], high)

    def uw_down():
        return remote(uw.at[1], uw.at[rows + 1], uw_send.at[1], uw_recv.at[1], low)

    def src_copy():
        return remote(source, forcing, src_send, src_recv, partner)

    def start_both(up, down):
        @pl.when(has_high)
        def _():
            up.start()

        @pl.when(has_low)
        def _():
            down.start()

    def wait_both(up, down):
        @pl.when(has_low)
        def _():
            up.wait_recv()
            down.wait_send()

        @pl.when(has_high)
        def _():
            down.wait_recv()
            up.wait_send()

    def start_uw():
        @pl.when(is_flow)
        def _():
            start_both(uw_up(), uw_down())

    def each_row(body):
        def step(row, carry):
            body(row)
            return carry

        lax.fori_loop(0, rows, step, 0)

    for slot in range(2):
        for line in range(2):
            pv[slot, line] = jnp.zeros((2, nx, nz), jnp.float32)
            pv[slot, rows + 2 + line] = jnp.zeros((2, nx, nz), jnp.float32)
    uw[0] = jnp.zeros((2, nx, nz), jnp.float32)
    uw[rows + 1] = jnp.zeros((2, nx, nz), jnp.float32)

    def load(row):
        pv[0, row + 2] = pv_ref[row]
        uw[row + 1] = uw_ref[row]

    each_row(load)

    barrier = pltpu.get_barrier_semaphore()

    def greet(device):
        pl.semaphore_signal(barrier, inc=1, device_id=device, device_id_type=pl.DeviceIdType.MESH)

    greet(partner)

    @pl.when(has_low)
    def _():
        greet(low)

    @pl.when(has_high)
    def _():
        greet(high)

    pl.semaphore_wait(barrier, 1 + has_low.astype(jnp.int32) + has_high.astype(jnp.int32))

    def put_matrix(mat_x, mat_z):
        dxs[0], dxs[1] = split_parts(mat_x[...])
        dzs[0], dzs[1] = split_parts(mat_z[...])

    def operators(slot):
        def body(row):
            p, v, u, w = pv[slot, row + 2, 0], pv[slot, row + 2, 1], uw[row + 1, 0], uw[row + 1, 1]
            sx = dot_parts((dxs[0], dxs[1]), split_parts(jnp.concatenate([p, u, v, w], axis=1)))
            sz = dot_parts(split_parts(jnp.concatenate([p, w], axis=0)), (dzs[0], dzs[1]))
            sp, su, sv, sw = (sx[:, i * nz:(i + 1) * nz] for i in range(4))
            part[row, 0] = p - time_step * (mach_number * sp + su + sz[nx:])
            part[row, 1] = u - time_step * (mach_number * su + sp)
            part[row, 2] = v - (time_step * mach_number) * sv
            part[row, 3] = w - time_step * (mach_number * sw + sz[:nx])

        each_row(body)

    def add_forcing():
        def body(row):
            for i in range(3):
                part[row, i + 1] = part[row, i + 1] + time_step * forcing[row, i]

        each_row(body)

    def keep_uw():
        def body(row):
            uw[row + 1, 0] = part[row, 1]
            uw[row + 1, 1] = part[row, 3]

        each_row(body)

    def update_pv(slot):
        def body(row):
            def dy(field):
                ahead = pv[slot, row + 3, field] - pv[slot, row + 1, field]
                return (8.0 * ahead - (pv[slot, row + 4, field] - pv[slot, row, field])) / 12.0

            pv[1 - slot, row + 2, 0] = part[row, 0] - time_step * dy(1)
            pv[1 - slot, row + 2, 1] = part[row, 2] - time_step * dy(0)

        each_row(body)

    def lamb_rows():
        def body(row):
            u, v, w = uw[row + 1, 0], pv[0, row + 2, 1], uw[row + 1, 1]
            ox = 0.5 * (uw[row + 2, 1] - uw[row, 1]) - inner_slope(v, 1)
            oy = inner_slope(u, 1) - inner_slope(w, 0)
            oz = inner_slope(v, 0) - 0.5 * (uw[row + 2, 0] - uw[row, 0])
            mask = -region_ref[row]
            source[row, 0] = mask * (oy * w - oz * v)
            source[row, 1] = mask * (oz * u - ox * w)
            source[row, 2] = mask * (ox * v - oy * u)

        each_row(body)

    def keep_edge(slot):
        edge[0] = pv[slot, 1, 0]
        edge[1] = pv[slot, rows + 2, 0]

    def advance_edges():
        def body(which, carry):
            row = which * (rows + 1)
            p, u, w = edge[which], uw[row, 0], uw[row, 1]
            sx = dot_parts((dxs[0], dxs[1]), split_parts(jnp.concatenate([p, u, w], axis=1)))
            sz = dot_parts(split_parts(p), (dzs[0], dzs[1]))
            sp, su, sw = (sx[:, i * nz:(i + 1) * nz] for i in range(3))
            uw[row, 0] = u - time_step * (mach_number * su + sp)
            uw[row, 1] = w - time_step * (mach_number * sw + sz)
            return carry

        @pl.when(is_flow)
        def _():
            lax.fori_loop(0, 2, body, 0)

    put_matrix(dx_ref, dzt_ref)
    start_uw()
    start_both(pv_up(0), pv_down(0))
    pairs = SEGMENTS // 2

    def pair(m, carry):
        @pl.when(is_flow)
        def _():
            @pl.when(m == 0)
            def _():
                wait_both(uw_up(), uw_down())

            lamb_rows()

            @pl.when(m > 0)
            def _():
                pl.semaphore_wait(credit, 1)

            src_copy().start()

        operators(0)

        @pl.when(is_sound)
        def _():
            src_copy().wait_recv()
            add_forcing()

        wait_both(pv_up(0), pv_down(0))
        update_pv(0)
        keep_edge(0)
        start_both(pv_up(1), pv_down(1))
        keep_uw()
        operators(1)

        @pl.when(is_sound)
        def _():
            add_forcing()

            @pl.when(m < pairs - 1)
            def _():
                pl.semaphore_signal(credit, inc=1, device_id=partner, device_id_type=pl.DeviceIdType.MESH)

        @pl.when(is_flow)
        def _():
            src_copy().wait_send()

        keep_uw()
        advance_edges()
        wait_both(pv_up(1), pv_down(1))
        update_pv(1)

        @pl.when(m < pairs - 1)
        def _():
            keep_edge(1)
            start_both(pv_up(0), pv_down(0))
            advance_edges()

        return carry

    lax.fori_loop(0, pairs, pair, 0)

    put_matrix(fx_ref, fzt_ref)

    def smooth(row):
        group = (pv[0, row + 2, 0], uw[row + 1, 0], pv[0, row + 2, 1], uw[row + 1, 1])
        sx = dot_parts((dxs[0], dxs[1]), split_parts(jnp.concatenate(group, axis=1)))
        sz = dot_parts(split_parts(jnp.concatenate(group, axis=0)), (dzs[0], dzs[1]))
        for i in range(4):
            out_ref[row, i] = group[i] + filter_weight * (sx[:, i * nz:(i + 1) * nz] + sz[i * nx:(i + 1) * nx])

    each_row(smooth)


def steps_call(streams, slabs, fields, region, deriv_x, deriv_zt, filter_x, filter_zt):
    rows, count, nx, nz = fields.shape
    pv = jnp.stack([fields[:, 0], fields[:, 2]], axis=1)
    uw = jnp.stack([fields[:, 1], fields[:, 3]], axis=1)
    f32 = jnp.float32
    dma = pltpu.SemaphoreType.DMA
    return pl.pallas_call(
        functools.partial(steps_kernel, streams, slabs),
        out_shape=jax.ShapeDtypeStruct(fields.shape, f32),
        in_specs=[pl.BlockSpec(memory_space=pltpu.VMEM)] * 7,
        out_specs=pl.BlockSpec(memory_space=pltpu.VMEM),
        scratch_shapes=[
            pltpu.VMEM((2, rows + 4, 2, nx, nz), f32),
            pltpu.VMEM((rows + 2, 2, nx, nz), f32),
            pltpu.VMEM((2, nx, nz), f32),
            pltpu.VMEM((rows, 4, nx, nz), f32),
            pltpu.VMEM((rows, 3, nx, nz), f32),
            pltpu.VMEM((rows, 3, nx, nz), f32),
            pltpu.VMEM((2, nx, nx), jnp.bfloat16),
            pltpu.VMEM((2, nz, nz), jnp.bfloat16),
            dma((2, 2)), dma((2, 2)), dma((2,)), dma((2,)), dma, dma,
            pltpu.SemaphoreType.REGULAR,
        ],
        compiler_params=pltpu.CompilerParams(
            collective_id=0, has_side_effects=True, vmem_limit_bytes=48 * 1024 * 1024
        ),
    )(pv, uw, jnp.broadcast_to(region, (rows, nx, nz)), deriv_x, deriv_zt, filter_x, filter_zt)


def plain_steps(order, fields, region, deriv_x, deriv_zt, filter_x, filter_zt):
    rows = fields.shape[0]
    forcing = None
    for segment in range(SEGMENTS):
        pv = jnp.stack([fields[:, 0], fields[:, 2]], axis=1)
        before, after = neighbour_rows(pv, 2, order, 2)
        if segment % 2 == 0:
            uw = jnp.stack([fields[:, 1], fields[:, 3]], axis=1)
            low, high = neighbour_rows(uw, 1, order, 1)
            source = -region * lamb(fields, low, high)
            forcing = lax.ppermute(source, "section", [(0, 1)])
        part = row_call(local_kernel, fields, deriv_x, deriv_zt)
        near = jnp.concatenate([before, pv, after], axis=0)
        dy = (8.0 * (near[3:3 + rows] - near[1:1 + rows]) - (near[4:4 + rows] - near[:rows])) / 12.0
        fields = jnp.stack(
            [
                part[:, 0] - time_step * dy[:, 1],
                part[:, 1] + time_step * forcing[:, 0],
                part[:, 2] + time_step * (forcing[:, 1] - dy[:, 0]),
                part[:, 3] + time_step * forcing[:, 2],
            ],
            axis=1,
        )
    return row_call(filter_kernel, fields, filter_x, filter_zt)


def shards(state, source_mask, deriv_x, deriv_z, filter_x, filter_z):
    streams, slabs = lax.axis_size("stream"), lax.axis_size("slab")
    place, order = chain(streams, slabs)
    fields = state[0]
    count, width_x, width_y, nz = fields.shape
    nx = width_x * streams
    rows = width_y // streams
    even = lax.axis_index("slab") % 2 == 0
    back = [streams - 1 - p for p in place]

    parts = fields.reshape(count, width_x, streams, rows, nz).transpose(2, 3, 0, 1, 4)
    parts = jnp.where(even, jnp.stack([parts[p] for p in place]), jnp.stack([parts[p] for p in back]))
    parts = lax.all_to_all(parts, "stream", split_axis=0, concat_axis=0, tiled=True)
    fields = parts.transpose(1, 2, 0, 3, 4).reshape(rows, count, nx, nz)

    blocks = source_mask.astype(jnp.float32)
    region = jnp.repeat(jnp.repeat(blocks, MBLK, axis=0), MBLK, axis=1).T
    mine = jnp.asarray(place)[lax.axis_index("stream")]
    mine = jnp.where(even, mine, streams - 1 - mine)
    region = lax.dynamic_slice_in_dim(region, mine * rows, rows, 0)[:, None, :, None]
    deriv_zt, filter_zt = deriv_z.T, filter_z.T

    mats = (deriv_x, deriv_zt, filter_x, filter_zt)
    if rows >= 2:
        fields = steps_call(streams, slabs, fields, region[:, 0], *mats)
    else:
        fields = plain_steps(order, fields, region, *mats)

    parts = fields.reshape(rows, count, streams, width_x, nz).transpose(2, 0, 1, 3, 4)
    parts = lax.all_to_all(parts, "stream", split_axis=0, concat_axis=0, tiled=True)
    inv_place = [place.index(j) for j in range(streams)]
    inv_back = [back.index(j) for j in range(streams)]
    parts = jnp.where(even, jnp.stack([parts[p] for p in inv_place]), jnp.stack([parts[p] for p in inv_back]))
    return parts.transpose(2, 3, 0, 1, 4).reshape(1, count, width_x, width_y, nz)


def solution(mesh):
    placed = (P("section", None, "stream", "slab", None), P(None, "slab"), P(), P(), P(), P())
    return jax.shard_map(
        shards,
        mesh=mesh,
        in_specs=placed,
        out_specs=P("section", None, "stream", "slab", None),
        check_vma=False,
    )
```

```python
import functools
import math

import jax
import jax.numpy as jnp
from jax import lax
from jax.experimental import pallas as pl
from jax.experimental.pallas import tpu as pltpu
from jax.sharding import PartitionSpec as P

SEGMENTS = 8
MBLK = 16

mach_number = 0.5
time_step = 0.05
filter_weight = 0.25


def split_parts(value):
    high = value.astype(jnp.bfloat16)
    low = (value - high.astype(jnp.float32)).astype(jnp.bfloat16)
    return high, low


def dot_parts(left, right):
    dot = functools.partial(jnp.dot, preferred_element_type=jnp.float32)
    return dot(left[0], right[0]) + (dot(left[0], right[1]) + dot(left[1], right[0]))


def wide(ref):
    return jnp.concatenate([ref[0, i] for i in range(4)], axis=1)


def local_kernel(fields_ref, dx_ref, dzt_ref, out_ref):
    nz = fields_ref.shape[3]
    nx = fields_ref.shape[2]
    dx = split_parts(dx_ref[...])
    dzt = split_parts(dzt_ref[...])
    fields = wide(fields_ref)
    sx = dot_parts(dx, split_parts(fields))
    sz = dot_parts(split_parts(jnp.concatenate([fields_ref[0, 0], fields_ref[0, 3]], axis=0)), dzt)
    sp, su, sv, sw = (sx[:, i * nz:(i + 1) * nz] for i in range(4))
    out_ref[0, 0] = fields_ref[0, 0] - time_step * (mach_number * sp + su + sz[nx:])
    out_ref[0, 1] = fields_ref[0, 1] - time_step * (mach_number * su + sp)
    out_ref[0, 2] = fields_ref[0, 2] - (time_step * mach_number) * sv
    out_ref[0, 3] = fields_ref[0, 3] - time_step * (mach_number * sw + sz[:nx])


def filter_kernel(fields_ref, fx_ref, fzt_ref, out_ref):
    nz = fields_ref.shape[3]
    nx = fields_ref.shape[2]
    fx = split_parts(fx_ref[...])
    fzt = split_parts(fzt_ref[...])
    sx = dot_parts(fx, split_parts(wide(fields_ref)))
    sz = dot_parts(split_parts(jnp.concatenate([fields_ref[0, i] for i in range(4)], axis=0)), fzt)
    for i in range(4):
        out_ref[0, i] = fields_ref[0, i] + filter_weight * (sx[:, i * nz:(i + 1) * nz] + sz[i * nx:(i + 1) * nx])


def row_call(kernel, fields, mat_x, mat_zt):
    rows, count, nx, nz = fields.shape
    block = pl.BlockSpec((1, count, nx, nz), lambda i: (i, 0, 0, 0))
    return pl.pallas_call(
        kernel,
        grid=(rows,),
        in_specs=[block, pl.BlockSpec((nx, nx), lambda i: (0, 0)), pl.BlockSpec((nz, nz), lambda i: (0, 0))],
        out_specs=block,
        out_shape=jax.ShapeDtypeStruct(fields.shape, jnp.float32),
        cost_estimate=pl.CostEstimate(
            flops=6 * rows * count * nx * nz * (nx + nz), bytes_accessed=8 * fields.size, transcendentals=0
        ),
    )(fields, mat_x, mat_zt)


def chain(streams, slabs):
    side = math.isqrt(streams)
    path = list(range(streams))
    if side * side == streams:
        path = [r * side + (c if r % 2 == 0 else side - 1 - c) for r in range(side) for c in range(side)]
    place = [path.index(s) for s in range(streams)]
    order = []
    for k in range(slabs):
        order += [s * slabs + k for s in (path if k % 2 == 0 else path[::-1])]
    return place, order


def neighbour_rows(values, width, order, sections):
    rows = values.shape[0]
    total = len(order)
    axes = ("section", "stream", "slab")

    def shift(part, steps):
        pairs = []
        for section in range(sections):
            for g in range(total):
                if 0 <= g + steps < total:
                    pairs.append((section * total + order[g], section * total + order[g + steps]))
        return lax.ppermute(part, axes, pairs)

    if rows >= width:
        return shift(values[rows - width:], 1), shift(values[:width], -1)
    reach = -(-width // rows)
    before = jnp.concatenate([shift(values, d) for d in range(reach, 0, -1)], axis=0)
    after = jnp.concatenate([shift(values, -d) for d in range(1, reach + 1)], axis=0)
    return before[reach * rows - width:], after[:width]


def slope(values, dim):
    pads = [(0, 0)] * values.ndim
    pads[dim] = (1, 1)
    padded = jnp.pad(values, pads)
    length = values.shape[dim]
    return 0.5 * (
        lax.slice_in_dim(padded, 2, length + 2, axis=dim) - lax.slice_in_dim(padded, 0, length, axis=dim)
    )


def lamb(fields, before, after):
    u, v, w = fields[:, 1], fields[:, 2], fields[:, 3]
    rows = fields.shape[0]
    near = jnp.concatenate([before, jnp.stack([u, w], axis=1), after], axis=0)
    c2 = 0.5 * (near[2:] - near[:rows])
    ox = c2[:, 1] - slope(v, 2)
    oy = slope(u, 2) - slope(w, 1)
    oz = slope(v, 1) - c2[:, 0]
    return jnp.stack([oy * w - oz * v, oz * u - ox * w, ox * v - oy * u], axis=1)


def shift_masked(value, dim, step):
    size = value.shape[dim]
    moved = pltpu.roll(value, (-step) % size, dim)
    index = lax.broadcasted_iota(jnp.int32, value.shape, dim)
    return jnp.where(index == (size - 1 if step > 0 else 0), 0.0, moved)


def inner_slope(value, dim):
    return 0.5 * (shift_masked(value, dim, 1) - shift_masked(value, dim, -1))


def fold(index, side):
    row = index // side
    col = index % side
    return row * side + col + (row % 2) * (side - 1 - 2 * col)


def steps_kernel(streams, slabs, pv_ref, uw_ref, region_ref, dx_ref, dzt_ref, fx_ref, fzt_ref, out_ref,
                 pv, uw, edge, part, source, forcing, dxs, dzs, pv_send, pv_recv, uw_send, uw_recv, src_send, src_recv, row_send, row_recv, credit):
    rows, _, nx, nz = pv_ref.shape
    total = streams * slabs
    side = math.isqrt(streams)
    side = side if side * side == streams else streams
    section, stream, slab = lax.axis_index("section"), lax.axis_index("stream"), lax.axis_index("slab")

    def turn(place, which):
        return place + (which % 2) * (streams - 1 - 2 * place)

    def device_at(spot):
        which = spot // streams
        return (section, fold(turn(spot % streams, which), side), which)

    spot = slab * streams + turn(fold(stream, side), slab)
    has_low, has_high = spot > 0, spot < total - 1
    low = device_at(jnp.maximum(spot - 1, 0))
    high = device_at(jnp.minimum(spot + 1, total - 1))
    partner = (1 - section, stream, slab)
    is_flow, is_sound = section == 0, section == 1

    def remote(src, dst, send, recv, device):
        return pltpu.make_async_remote_copy(
            src_ref=src, dst_ref=dst, send_sem=send, recv_sem=recv,
            device_id=device, device_id_type=pl.DeviceIdType.MESH,
        )

    def pv_up(slot):
        return remote(pv.at[slot, pl.ds(rows, 2)], pv.at[slot, pl.ds(0, 2)], pv_send.at[slot, 0], pv_recv.at[slot, 0], high)

    def pv_down(slot):
        return remote(pv.at[slot, pl.ds(2, 2)], pv.at[slot, pl.ds(rows + 2, 2)], pv_send.at[slot, 1], pv_recv.at[slot, 1], low)

    def uw_up():
        return remote(uw.at[rows], uw.at[0], uw_send.at[0], uw_recv.at[0], high)

    def uw_down():
        return remote(uw.at[1], uw.at[rows + 1], uw_send.at[1], uw_recv.at[1], low)

    def src_copy():
        return remote(source, forcing, src_send, src_recv, partner)

    def start_both(up, down):
        @pl.when(has_high)
        def _():
            up.start()

        @pl.when(has_low)
        def _():
            down.start()

    def wait_both(up, down):
        @pl.when(has_low)
        def _():
            up.wait_recv()
            down.wait_send()

        @pl.when(has_high)
        def _():
            down.wait_recv()
            up.wait_send()

    def start_uw():
        @pl.when(is_flow)
        def _():
            start_both(uw_up(), uw_down())

    def each_row(body):
        def step(row, carry):
            body(row)
            return carry

        lax.fori_loop(0, rows, step, 0)

    for slot in range(2):
        for line in range(2):
            pv[slot, line] = jnp.zeros((2, nx, nz), jnp.float32)
            pv[slot, rows + 2 + line] = jnp.zeros((2, nx, nz), jnp.float32)
    uw[0] = jnp.zeros((2, nx, nz), jnp.float32)
    uw[rows + 1] = jnp.zeros((2, nx, nz), jnp.float32)

    def load(row):
        pv[0, row + 2] = pv_ref[row]
        uw[row + 1] = uw_ref[row]

    each_row(load)

    barrier = pltpu.get_barrier_semaphore()

    def greet(device):
        pl.semaphore_signal(barrier, inc=1, device_id=device, device_id_type=pl.DeviceIdType.MESH)

    greet(partner)
    for t in range(1, streams):
        greet((section, (stream + t) % streams, slab))
    low_apart = has_low & (spot % streams == 0)
    high_apart = has_high & (spot % streams == streams - 1)

    @pl.when(low_apart)
    def _():
        greet(low)

    @pl.when(high_apart)
    def _():
        greet(high)

    pl.semaphore_wait(barrier, streams + low_apart.astype(jnp.int32) + high_apart.astype(jnp.int32))

    def put_matrix(mat_x, mat_z):
        dxs[0], dxs[1] = split_parts(mat_x[...])
        dzs[0], dzs[1] = split_parts(mat_z[...])

    def operators(slot):
        def body(row):
            p, v, u, w = pv[slot, row + 2, 0], pv[slot, row + 2, 1], uw[row + 1, 0], uw[row + 1, 1]
            sx = dot_parts((dxs[0], dxs[1]), split_parts(jnp.concatenate([p, u, v, w], axis=1)))
            sz = dot_parts(split_parts(jnp.concatenate([p, w], axis=0)), (dzs[0], dzs[1]))
            sp, su, sv, sw = (sx[:, i * nz:(i + 1) * nz] for i in range(4))
            part[row, 0] = p - time_step * (mach_number * sp + su + sz[nx:])
            part[row, 1] = u - time_step * (mach_number * su + sp)
            part[row, 2] = v - (time_step * mach_number) * sv
            part[row, 3] = w - time_step * (mach_number * sw + sz[:nx])

        each_row(body)

    def add_forcing():
        def body(row):
            for i in range(3):
                part[row, i + 1] = part[row, i + 1] + time_step * forcing[row, i]

        each_row(body)

    def keep_uw():
        def body(row):
            uw[row + 1, 0] = part[row, 1]
            uw[row + 1, 1] = part[row, 3]

        each_row(body)

    def update_pv(slot):
        def body(row):
            def dy(field):
                ahead = pv[slot, row + 3, field] - pv[slot, row + 1, field]
                return (8.0 * ahead - (pv[slot, row + 4, field] - pv[slot, row, field])) / 12.0

            pv[1 - slot, row + 2, 0] = part[row, 0] - time_step * dy(1)
            pv[1 - slot, row + 2, 1] = part[row, 2] - time_step * dy(0)

        each_row(body)

    def lamb_rows():
        def body(row):
            u, v, w = uw[row + 1, 0], pv[0, row + 2, 1], uw[row + 1, 1]
            ox = 0.5 * (uw[row + 2, 1] - uw[row, 1]) - inner_slope(v, 1)
            oy = inner_slope(u, 1) - inner_slope(w, 0)
            oz = inner_slope(v, 0) - 0.5 * (uw[row + 2, 0] - uw[row, 0])
            mask = -region_ref[row]
            source[row, 0] = mask * (oy * w - oz * v)
            source[row, 1] = mask * (oz * u - ox * w)
            source[row, 2] = mask * (ox * v - oy * u)

        each_row(body)

    def keep_edge(slot):
        edge[0] = pv[slot, 1, 0]
        edge[1] = pv[slot, rows + 2, 0]

    def advance_edges():
        def body(which, carry):
            row = which * (rows + 1)
            p, u, w = edge[which], uw[row, 0], uw[row, 1]
            sx = dot_parts((dxs[0], dxs[1]), split_parts(jnp.concatenate([p, u, w], axis=1)))
            sz = dot_parts(split_parts(p), (dzs[0], dzs[1]))
            sp, su, sw = (sx[:, i * nz:(i + 1) * nz] for i in range(3))
            uw[row, 0] = u - time_step * (mach_number * su + sp)
            uw[row, 1] = w - time_step * (mach_number * sw + sz)
            return carry

        @pl.when(is_flow)
        def _():
            lax.fori_loop(0, 2, body, 0)

    put_matrix(dx_ref, dzt_ref)
    start_uw()
    start_both(pv_up(0), pv_down(0))
    pairs = SEGMENTS // 2

    def pair(m, carry):
        @pl.when(is_flow)
        def _():
            @pl.when(m == 0)
            def _():
                wait_both(uw_up(), uw_down())

            lamb_rows()

            @pl.when(m > 0)
            def _():
                pl.semaphore_wait(credit, 1)

            src_copy().start()

        operators(0)

        @pl.when(is_sound)
        def _():
            src_copy().wait_recv()
            add_forcing()

        wait_both(pv_up(0), pv_down(0))
        update_pv(0)
        keep_edge(0)
        start_both(pv_up(1), pv_down(1))
        keep_uw()
        operators(1)

        @pl.when(is_sound)
        def _():
            add_forcing()

            @pl.when(m < pairs - 1)
            def _():
                pl.semaphore_signal(credit, inc=1, device_id=partner, device_id_type=pl.DeviceIdType.MESH)

        @pl.when(is_flow)
        def _():
            src_copy().wait_send()

        keep_uw()
        advance_edges()
        wait_both(pv_up(1), pv_down(1))
        update_pv(1)

        @pl.when(m < pairs - 1)
        def _():
            keep_edge(1)
            start_both(pv_up(0), pv_down(0))
            advance_edges()

        return carry

    lax.fori_loop(0, pairs, pair, 0)

    put_matrix(fx_ref, fzt_ref)

    def smooth(row):
        group = (pv[0, row + 2, 0], uw[row + 1, 0], pv[0, row + 2, 1], uw[row + 1, 1])
        sx = dot_parts((dxs[0], dxs[1]), split_parts(jnp.concatenate(group, axis=1)))
        sz = dot_parts(split_parts(jnp.concatenate(group, axis=0)), (dzs[0], dzs[1]))
        for i in range(4):
            part[row, i] = group[i] + filter_weight * (sx[:, i * nz:(i + 1) * nz] + sz[i * nx:(i + 1) * nx])
        for t in range(1, streams):
            row_copy(t, row).start()
        own = pl.ds(pl.multiple_of(stream * width, width), width)
        out_ref[chunk_of(stream), row] = part[row, :, own]

    width = nx // streams

    def chunk_of(which):
        return turn(fold(which, side), slab)

    def row_copy(t, row):
        peer = (stream + t) % streams
        cells = pl.ds(pl.multiple_of(peer * width, width), width)
        return remote(
            part.at[row, :, cells], out_ref.at[chunk_of(stream), row],
            row_send.at[t - 1, row], row_recv.at[t - 1, row], (section, peer, slab),
        )

    each_row(smooth)

    def finish(row):
        for t in range(1, streams):
            sender = (stream + streams - t) % streams
            landed = out_ref.at[chunk_of(sender), row]
            row_copy(t, row).wait_send()
            remote(landed, landed, row_send.at[t - 1, row], row_recv.at[t - 1, row], (section, sender, slab)).wait_recv()

    each_row(finish)


def steps_call(streams, slabs, fields, region, deriv_x, deriv_zt, filter_x, filter_zt):
    rows, count, nx, nz = fields.shape
    pv = jnp.stack([fields[:, 0], fields[:, 2]], axis=1)
    uw = jnp.stack([fields[:, 1], fields[:, 3]], axis=1)
    f32 = jnp.float32
    dma = pltpu.SemaphoreType.DMA
    return pl.pallas_call(
        functools.partial(steps_kernel, streams, slabs),
        out_shape=jax.ShapeDtypeStruct((streams, rows, count, nx // streams, nz), f32),
        in_specs=[pl.BlockSpec(memory_space=pltpu.VMEM)] * 7,
        out_specs=pl.BlockSpec(memory_space=pltpu.VMEM),
        scratch_shapes=[
            pltpu.VMEM((2, rows + 4, 2, nx, nz), f32),
            pltpu.VMEM((rows + 2, 2, nx, nz), f32),
            pltpu.VMEM((2, nx, nz), f32),
            pltpu.VMEM((rows, 4, nx, nz), f32),
            pltpu.VMEM((rows, 3, nx, nz), f32),
            pltpu.VMEM((rows, 3, nx, nz), f32),
            pltpu.VMEM((2, nx, nx), jnp.bfloat16),
            pltpu.VMEM((2, nz, nz), jnp.bfloat16),
            dma((2, 2)), dma((2, 2)), dma((2,)), dma((2,)), dma, dma,
            dma((streams - 1, rows)), dma((streams - 1, rows)),
            pltpu.SemaphoreType.REGULAR,
        ],
        compiler_params=pltpu.CompilerParams(
            collective_id=0, has_side_effects=True, vmem_limit_bytes=48 * 1024 * 1024
        ),
    )(pv, uw, jnp.broadcast_to(region, (rows, nx, nz)), deriv_x, deriv_zt, filter_x, filter_zt)


def plain_steps(order, fields, region, deriv_x, deriv_zt, filter_x, filter_zt):
    rows = fields.shape[0]
    forcing = None
    for segment in range(SEGMENTS):
        pv = jnp.stack([fields[:, 0], fields[:, 2]], axis=1)
        before, after = neighbour_rows(pv, 2, order, 2)
        if segment % 2 == 0:
            uw = jnp.stack([fields[:, 1], fields[:, 3]], axis=1)
            low, high = neighbour_rows(uw, 1, order, 1)
            source = -region * lamb(fields, low, high)
            forcing = lax.ppermute(source, "section", [(0, 1)])
        part = row_call(local_kernel, fields, deriv_x, deriv_zt)
        near = jnp.concatenate([before, pv, after], axis=0)
        dy = (8.0 * (near[3:3 + rows] - near[1:1 + rows]) - (near[4:4 + rows] - near[:rows])) / 12.0
        fields = jnp.stack(
            [
                part[:, 0] - time_step * dy[:, 1],
                part[:, 1] + time_step * forcing[:, 0],
                part[:, 2] + time_step * (forcing[:, 1] - dy[:, 0]),
                part[:, 3] + time_step * forcing[:, 2],
            ],
            axis=1,
        )
    return row_call(filter_kernel, fields, filter_x, filter_zt)


def shards(state, source_mask, deriv_x, deriv_z, filter_x, filter_z):
    streams, slabs = lax.axis_size("stream"), lax.axis_size("slab")
    place, order = chain(streams, slabs)
    fields = state[0]
    count, width_x, width_y, nz = fields.shape
    nx = width_x * streams
    rows = width_y // streams
    even = lax.axis_index("slab") % 2 == 0
    back = [streams - 1 - p for p in place]

    parts = fields.reshape(count, width_x, streams, rows, nz).transpose(2, 3, 0, 1, 4)
    parts = jnp.where(even, jnp.stack([parts[p] for p in place]), jnp.stack([parts[p] for p in back]))
    parts = lax.all_to_all(parts, "stream", split_axis=0, concat_axis=0, tiled=True)
    fields = parts.transpose(1, 2, 0, 3, 4).reshape(rows, count, nx, nz)

    blocks = source_mask.astype(jnp.float32)
    region = jnp.repeat(jnp.repeat(blocks, MBLK, axis=0), MBLK, axis=1).T
    mine = jnp.asarray(place)[lax.axis_index("stream")]
    mine = jnp.where(even, mine, streams - 1 - mine)
    region = lax.dynamic_slice_in_dim(region, mine * rows, rows, 0)[:, None, :, None]
    deriv_zt, filter_zt = deriv_z.T, filter_z.T

    mats = (deriv_x, deriv_zt, filter_x, filter_zt)
    if rows >= 2:
        parts = steps_call(streams, slabs, fields, region[:, 0], *mats)
        return parts.transpose(2, 3, 0, 1, 4).reshape(1, count, width_x, width_y, nz)
    fields = plain_steps(order, fields, region, *mats)

    parts = fields.reshape(rows, count, streams, width_x, nz).transpose(2, 0, 1, 3, 4)
    parts = lax.all_to_all(parts, "stream", split_axis=0, concat_axis=0, tiled=True)
    inv_place = [place.index(j) for j in range(streams)]
    inv_back = [back.index(j) for j in range(streams)]
    parts = jnp.where(even, jnp.stack([parts[p] for p in inv_place]), jnp.stack([parts[p] for p in inv_back]))
    return parts.transpose(2, 3, 0, 1, 4).reshape(1, count, width_x, width_y, nz)


def solution(mesh):
    placed = (P("section", None, "stream", "slab", None), P(None, "slab"), P(), P(), P(), P())
    return jax.shard_map(
        shards,
        mesh=mesh,
        in_specs=placed,
        out_specs=P("section", None, "stream", "slab", None),
        check_vma=False,
    )
```

```python
import functools
import math

import jax
import jax.numpy as jnp
from jax import lax
from jax.experimental import pallas as pl
from jax.experimental.pallas import tpu as pltpu
from jax.sharding import PartitionSpec as P

SEGMENTS = 8
MBLK = 16

mach_number = 0.5
time_step = 0.05
filter_weight = 0.25


def split_parts(value):
    high = value.astype(jnp.bfloat16)
    low = (value - high.astype(jnp.float32)).astype(jnp.bfloat16)
    return high, low


def dot_parts(left, right):
    dot = functools.partial(jnp.dot, preferred_element_type=jnp.float32)
    return dot(left[0], right[0]) + (dot(left[0], right[1]) + dot(left[1], right[0]))


def wide(ref):
    return jnp.concatenate([ref[0, i] for i in range(4)], axis=1)


def local_kernel(fields_ref, dx_ref, dzt_ref, out_ref):
    nz = fields_ref.shape[3]
    nx = fields_ref.shape[2]
    dx = split_parts(dx_ref[...])
    dzt = split_parts(dzt_ref[...])
    fields = wide(fields_ref)
    sx = dot_parts(dx, split_parts(fields))
    sz = dot_parts(split_parts(jnp.concatenate([fields_ref[0, 0], fields_ref[0, 3]], axis=0)), dzt)
    sp, su, sv, sw = (sx[:, i * nz:(i + 1) * nz] for i in range(4))
    out_ref[0, 0] = fields_ref[0, 0] - time_step * (mach_number * sp + su + sz[nx:])
    out_ref[0, 1] = fields_ref[0, 1] - time_step * (mach_number * su + sp)
    out_ref[0, 2] = fields_ref[0, 2] - (time_step * mach_number) * sv
    out_ref[0, 3] = fields_ref[0, 3] - time_step * (mach_number * sw + sz[:nx])


def filter_kernel(fields_ref, fx_ref, fzt_ref, out_ref):
    nz = fields_ref.shape[3]
    nx = fields_ref.shape[2]
    fx = split_parts(fx_ref[...])
    fzt = split_parts(fzt_ref[...])
    sx = dot_parts(fx, split_parts(wide(fields_ref)))
    sz = dot_parts(split_parts(jnp.concatenate([fields_ref[0, i] for i in range(4)], axis=0)), fzt)
    for i in range(4):
        out_ref[0, i] = fields_ref[0, i] + filter_weight * (sx[:, i * nz:(i + 1) * nz] + sz[i * nx:(i + 1) * nx])


def row_call(kernel, fields, mat_x, mat_zt):
    rows, count, nx, nz = fields.shape
    block = pl.BlockSpec((1, count, nx, nz), lambda i: (i, 0, 0, 0))
    return pl.pallas_call(
        kernel,
        grid=(rows,),
        in_specs=[block, pl.BlockSpec((nx, nx), lambda i: (0, 0)), pl.BlockSpec((nz, nz), lambda i: (0, 0))],
        out_specs=block,
        out_shape=jax.ShapeDtypeStruct(fields.shape, jnp.float32),
        cost_estimate=pl.CostEstimate(
            flops=6 * rows * count * nx * nz * (nx + nz), bytes_accessed=8 * fields.size, transcendentals=0
        ),
    )(fields, mat_x, mat_zt)


def chain(streams, slabs):
    side = math.isqrt(streams)
    path = list(range(streams))
    if side * side == streams:
        path = [r * side + (c if r % 2 == 0 else side - 1 - c) for r in range(side) for c in range(side)]
    place = [path.index(s) for s in range(streams)]
    order = []
    for k in range(slabs):
        order += [s * slabs + k for s in (path if k % 2 == 0 else path[::-1])]
    return place, order


def neighbour_rows(values, width, order, sections):
    rows = values.shape[0]
    total = len(order)
    axes = ("section", "stream", "slab")

    def shift(part, steps):
        pairs = []
        for section in range(sections):
            for g in range(total):
                if 0 <= g + steps < total:
                    pairs.append((section * total + order[g], section * total + order[g + steps]))
        return lax.ppermute(part, axes, pairs)

    if rows >= width:
        return shift(values[rows - width:], 1), shift(values[:width], -1)
    reach = -(-width // rows)
    before = jnp.concatenate([shift(values, d) for d in range(reach, 0, -1)], axis=0)
    after = jnp.concatenate([shift(values, -d) for d in range(1, reach + 1)], axis=0)
    return before[reach * rows - width:], after[:width]


def slope(values, dim):
    pads = [(0, 0)] * values.ndim
    pads[dim] = (1, 1)
    padded = jnp.pad(values, pads)
    length = values.shape[dim]
    return 0.5 * (
        lax.slice_in_dim(padded, 2, length + 2, axis=dim) - lax.slice_in_dim(padded, 0, length, axis=dim)
    )


def lamb(fields, before, after):
    u, v, w = fields[:, 1], fields[:, 2], fields[:, 3]
    rows = fields.shape[0]
    near = jnp.concatenate([before, jnp.stack([u, w], axis=1), after], axis=0)
    c2 = 0.5 * (near[2:] - near[:rows])
    ox = c2[:, 1] - slope(v, 2)
    oy = slope(u, 2) - slope(w, 1)
    oz = slope(v, 1) - c2[:, 0]
    return jnp.stack([oy * w - oz * v, oz * u - ox * w, ox * v - oy * u], axis=1)


def shift_masked(value, dim, step):
    size = value.shape[dim]
    moved = pltpu.roll(value, (-step) % size, dim)
    index = lax.broadcasted_iota(jnp.int32, value.shape, dim)
    return jnp.where(index == (size - 1 if step > 0 else 0), 0.0, moved)


def inner_slope(value, dim):
    return 0.5 * (shift_masked(value, dim, 1) - shift_masked(value, dim, -1))


def fold(index, side):
    row = index // side
    col = index % side
    return row * side + col + (row % 2) * (side - 1 - 2 * col)


def steps_kernel(streams, slabs, cells_ref, region_ref, dx_ref, dzt_ref, fx_ref, fzt_ref, out_ref,
                 pv, uw, edge, part, source, forcing, dxs, dzs, pv_send, pv_recv, uw_send, uw_recv, src_send, src_recv, row_send, row_recv, in_send, in_recv, credit):
    _, rows, _, width, nz = cells_ref.shape
    nx = width * streams
    total = streams * slabs
    side = math.isqrt(streams)
    side = side if side * side == streams else streams
    section, stream, slab = lax.axis_index("section"), lax.axis_index("stream"), lax.axis_index("slab")

    def turn(place, which):
        return place + (which % 2) * (streams - 1 - 2 * place)

    def device_at(spot):
        which = spot // streams
        return (section, fold(turn(spot % streams, which), side), which)

    spot = slab * streams + turn(fold(stream, side), slab)
    has_low, has_high = spot > 0, spot < total - 1
    low = device_at(jnp.maximum(spot - 1, 0))
    high = device_at(jnp.minimum(spot + 1, total - 1))
    partner = (1 - section, stream, slab)
    is_flow, is_sound = section == 0, section == 1

    def remote(src, dst, send, recv, device):
        return pltpu.make_async_remote_copy(
            src_ref=src, dst_ref=dst, send_sem=send, recv_sem=recv,
            device_id=device, device_id_type=pl.DeviceIdType.MESH,
        )

    def pv_up(slot):
        return remote(pv.at[slot, pl.ds(rows, 2)], pv.at[slot, pl.ds(0, 2)], pv_send.at[slot, 0], pv_recv.at[slot, 0], high)

    def pv_down(slot):
        return remote(pv.at[slot, pl.ds(2, 2)], pv.at[slot, pl.ds(rows + 2, 2)], pv_send.at[slot, 1], pv_recv.at[slot, 1], low)

    def uw_up():
        return remote(uw.at[rows], uw.at[0], uw_send.at[0], uw_recv.at[0], high)

    def uw_down():
        return remote(uw.at[1], uw.at[rows + 1], uw_send.at[1], uw_recv.at[1], low)

    def src_copy():
        return remote(source, forcing, src_send, src_recv, partner)

    def start_both(up, down):
        @pl.when(has_high)
        def _():
            up.start()

        @pl.when(has_low)
        def _():
            down.start()

    def wait_both(up, down):
        @pl.when(has_low)
        def _():
            up.wait_recv()
            down.wait_send()

        @pl.when(has_high)
        def _():
            down.wait_recv()
            up.wait_send()

    def start_uw():
        @pl.when(is_flow)
        def _():
            start_both(uw_up(), uw_down())

    def each_row(body):
        def step(row, carry):
            body(row)
            return carry

        lax.fori_loop(0, rows, step, 0)

    for slot in range(2):
        for line in range(2):
            pv[slot, line] = jnp.zeros((2, nx, nz), jnp.float32)
            pv[slot, rows + 2 + line] = jnp.zeros((2, nx, nz), jnp.float32)
    uw[0] = jnp.zeros((2, nx, nz), jnp.float32)
    uw[rows + 1] = jnp.zeros((2, nx, nz), jnp.float32)

    barrier = pltpu.get_barrier_semaphore()

    def greet(device):
        pl.semaphore_signal(barrier, inc=1, device_id=device, device_id_type=pl.DeviceIdType.MESH)

    greet(partner)
    for t in range(1, streams):
        greet((section, (stream + t) % streams, slab))
    low_apart = has_low & (spot % streams == 0)
    high_apart = has_high & (spot % streams == streams - 1)

    @pl.when(low_apart)
    def _():
        greet(low)

    @pl.when(high_apart)
    def _():
        greet(high)

    pl.semaphore_wait(barrier, streams + low_apart.astype(jnp.int32) + high_apart.astype(jnp.int32))

    def chunk_of(which):
        return turn(fold(which, side), slab)

    def axial(which):
        return pl.ds(pl.multiple_of(which * width, width), width)

    def in_copy(t):
        peer = (stream + t) % streams
        return remote(
            cells_ref.at[chunk_of(peer)], part.at[:, :, axial(stream)],
            in_send.at[t - 1], in_recv.at[t - 1], (section, peer, slab),
        )

    for t in range(1, streams):
        in_copy(t).start()
    part[:, :, axial(stream)] = cells_ref[chunk_of(stream)]
    for t in range(1, streams):
        sender = (stream + streams - t) % streams
        landed = part.at[:, :, axial(sender)]
        in_copy(t).wait_send()
        remote(landed, landed, in_send.at[t - 1], in_recv.at[t - 1], (section, sender, slab)).wait_recv()

    def load(row):
        pv[0, row + 2, 0] = part[row, 0]
        pv[0, row + 2, 1] = part[row, 2]
        uw[row + 1, 0] = part[row, 1]
        uw[row + 1, 1] = part[row, 3]

    each_row(load)

    def put_matrix(mat_x, mat_z):
        dxs[0], dxs[1] = split_parts(mat_x[...])
        dzs[0], dzs[1] = split_parts(mat_z[...])

    def operators(slot):
        def body(row):
            p, v, u, w = pv[slot, row + 2, 0], pv[slot, row + 2, 1], uw[row + 1, 0], uw[row + 1, 1]
            sx = dot_parts((dxs[0], dxs[1]), split_parts(jnp.concatenate([p, u, v, w], axis=1)))
            sz = dot_parts(split_parts(jnp.concatenate([p, w], axis=0)), (dzs[0], dzs[1]))
            sp, su, sv, sw = (sx[:, i * nz:(i + 1) * nz] for i in range(4))
            part[row, 0] = p - time_step * (mach_number * sp + su + sz[nx:])
            part[row, 1] = u - time_step * (mach_number * su + sp)
            part[row, 2] = v - (time_step * mach_number) * sv
            part[row, 3] = w - time_step * (mach_number * sw + sz[:nx])

        each_row(body)

    def add_forcing():
        def body(row):
            for i in range(3):
                part[row, i + 1] = part[row, i + 1] + time_step * forcing[row, i]

        each_row(body)

    def keep_uw():
        def body(row):
            uw[row + 1, 0] = part[row, 1]
            uw[row + 1, 1] = part[row, 3]

        each_row(body)

    def update_pv(slot):
        def body(row):
            def dy(field):
                ahead = pv[slot, row + 3, field] - pv[slot, row + 1, field]
                return (8.0 * ahead - (pv[slot, row + 4, field] - pv[slot, row, field])) / 12.0

            pv[1 - slot, row + 2, 0] = part[row, 0] - time_step * dy(1)
            pv[1 - slot, row + 2, 1] = part[row, 2] - time_step * dy(0)

        each_row(body)

    def lamb_rows():
        def body(row):
            u, v, w = uw[row + 1, 0], pv[0, row + 2, 1], uw[row + 1, 1]
            ox = 0.5 * (uw[row + 2, 1] - uw[row, 1]) - inner_slope(v, 1)
            oy = inner_slope(u, 1) - inner_slope(w, 0)
            oz = inner_slope(v, 0) - 0.5 * (uw[row + 2, 0] - uw[row, 0])
            mask = -region_ref[row]
            source[row, 0] = mask * (oy * w - oz * v)
            source[row, 1] = mask * (oz * u - ox * w)
            source[row, 2] = mask * (ox * v - oy * u)

        each_row(body)

    def keep_edge(slot):
        edge[0] = pv[slot, 1, 0]
        edge[1] = pv[slot, rows + 2, 0]

    def advance_edges():
        def body(which, carry):
            row = which * (rows + 1)
            p, u, w = edge[which], uw[row, 0], uw[row, 1]
            sx = dot_parts((dxs[0], dxs[1]), split_parts(jnp.concatenate([p, u, w], axis=1)))
            sz = dot_parts(split_parts(p), (dzs[0], dzs[1]))
            sp, su, sw = (sx[:, i * nz:(i + 1) * nz] for i in range(3))
            uw[row, 0] = u - time_step * (mach_number * su + sp)
            uw[row, 1] = w - time_step * (mach_number * sw + sz)
            return carry

        @pl.when(is_flow)
        def _():
            lax.fori_loop(0, 2, body, 0)

    put_matrix(dx_ref, dzt_ref)
    start_uw()
    start_both(pv_up(0), pv_down(0))
    pairs = SEGMENTS // 2

    def pair(m, carry):
        @pl.when(is_flow)
        def _():
            @pl.when(m == 0)
            def _():
                wait_both(uw_up(), uw_down())

            lamb_rows()

            @pl.when(m > 0)
            def _():
                pl.semaphore_wait(credit, 1)

            src_copy().start()

        operators(0)

        @pl.when(is_sound)
        def _():
            src_copy().wait_recv()
            add_forcing()

        wait_both(pv_up(0), pv_down(0))
        update_pv(0)
        keep_edge(0)
        start_both(pv_up(1), pv_down(1))
        keep_uw()
        operators(1)

        @pl.when(is_sound)
        def _():
            add_forcing()

            @pl.when(m < pairs - 1)
            def _():
                pl.semaphore_signal(credit, inc=1, device_id=partner, device_id_type=pl.DeviceIdType.MESH)

        @pl.when(is_flow)
        def _():
            src_copy().wait_send()

        keep_uw()
        advance_edges()
        wait_both(pv_up(1), pv_down(1))
        update_pv(1)

        @pl.when(m < pairs - 1)
        def _():
            keep_edge(1)
            start_both(pv_up(0), pv_down(0))
            advance_edges()

        return carry

    lax.fori_loop(0, pairs, pair, 0)

    put_matrix(fx_ref, fzt_ref)

    def smooth(row):
        group = (pv[0, row + 2, 0], uw[row + 1, 0], pv[0, row + 2, 1], uw[row + 1, 1])
        sx = dot_parts((dxs[0], dxs[1]), split_parts(jnp.concatenate(group, axis=1)))
        sz = dot_parts(split_parts(jnp.concatenate(group, axis=0)), (dzs[0], dzs[1]))
        for i in range(4):
            part[row, i] = group[i] + filter_weight * (sx[:, i * nz:(i + 1) * nz] + sz[i * nx:(i + 1) * nx])
        for t in range(1, streams):
            row_copy(t, row).start()
        own = pl.ds(pl.multiple_of(stream * width, width), width)
        out_ref[chunk_of(stream), row] = part[row, :, own]

    def row_copy(t, row):
        peer = (stream + t) % streams
        cells = pl.ds(pl.multiple_of(peer * width, width), width)
        return remote(
            part.at[row, :, cells], out_ref.at[chunk_of(stream), row],
            row_send.at[t - 1, row], row_recv.at[t - 1, row], (section, peer, slab),
        )

    each_row(smooth)

    def finish(row):
        for t in range(1, streams):
            sender = (stream + streams - t) % streams
            landed = out_ref.at[chunk_of(sender), row]
            row_copy(t, row).wait_send()
            remote(landed, landed, row_send.at[t - 1, row], row_recv.at[t - 1, row], (section, sender, slab)).wait_recv()

    each_row(finish)


def steps_call(streams, slabs, cells, region, deriv_x, deriv_zt, filter_x, filter_zt):
    _, rows, count, width, nz = cells.shape
    nx = width * streams
    f32 = jnp.float32
    dma = pltpu.SemaphoreType.DMA
    return pl.pallas_call(
        functools.partial(steps_kernel, streams, slabs),
        out_shape=jax.ShapeDtypeStruct((streams, rows, count, nx // streams, nz), f32),
        in_specs=[pl.BlockSpec(memory_space=pltpu.VMEM)] * 6,
        out_specs=pl.BlockSpec(memory_space=pltpu.VMEM),
        scratch_shapes=[
            pltpu.VMEM((2, rows + 4, 2, nx, nz), f32),
            pltpu.VMEM((rows + 2, 2, nx, nz), f32),
            pltpu.VMEM((2, nx, nz), f32),
            pltpu.VMEM((rows, 4, nx, nz), f32),
            pltpu.VMEM((rows, 3, nx, nz), f32),
            pltpu.VMEM((rows, 3, nx, nz), f32),
            pltpu.VMEM((2, nx, nx), jnp.bfloat16),
            pltpu.VMEM((2, nz, nz), jnp.bfloat16),
            dma((2, 2)), dma((2, 2)), dma((2,)), dma((2,)), dma, dma,
            dma((streams - 1, rows)), dma((streams - 1, rows)), dma((streams - 1,)), dma((streams - 1,)),
            pltpu.SemaphoreType.REGULAR,
        ],
        compiler_params=pltpu.CompilerParams(
            collective_id=0, has_side_effects=True, vmem_limit_bytes=48 * 1024 * 1024
        ),
    )(cells, jnp.broadcast_to(region, (rows, nx, nz)), deriv_x, deriv_zt, filter_x, filter_zt)


def plain_steps(order, fields, region, deriv_x, deriv_zt, filter_x, filter_zt):
    rows = fields.shape[0]
    forcing = None
    for segment in range(SEGMENTS):
        pv = jnp.stack([fields[:, 0], fields[:, 2]], axis=1)
        before, after = neighbour_rows(pv, 2, order, 2)
        if segment % 2 == 0:
            uw = jnp.stack([fields[:, 1], fields[:, 3]], axis=1)
            low, high = neighbour_rows(uw, 1, order, 1)
            source = -region * lamb(fields, low, high)
            forcing = lax.ppermute(source, "section", [(0, 1)])
        part = row_call(local_kernel, fields, deriv_x, deriv_zt)
        near = jnp.concatenate([before, pv, after], axis=0)
        dy = (8.0 * (near[3:3 + rows] - near[1:1 + rows]) - (near[4:4 + rows] - near[:rows])) / 12.0
        fields = jnp.stack(
            [
                part[:, 0] - time_step * dy[:, 1],
                part[:, 1] + time_step * forcing[:, 0],
                part[:, 2] + time_step * (forcing[:, 1] - dy[:, 0]),
                part[:, 3] + time_step * forcing[:, 2],
            ],
            axis=1,
        )
    return row_call(filter_kernel, fields, filter_x, filter_zt)


def shards(state, source_mask, deriv_x, deriv_z, filter_x, filter_z):
    streams, slabs = lax.axis_size("stream"), lax.axis_size("slab")
    place, order = chain(streams, slabs)
    fields = state[0]
    count, width_x, width_y, nz = fields.shape
    nx = width_x * streams
    rows = width_y // streams
    even = lax.axis_index("slab") % 2 == 0
    back = [streams - 1 - p for p in place]

    parts = fields.reshape(count, width_x, streams, rows, nz).transpose(2, 3, 0, 1, 4)
    blocks = source_mask.astype(jnp.float32)
    region = jnp.repeat(jnp.repeat(blocks, MBLK, axis=0), MBLK, axis=1).T
    mine = jnp.asarray(place)[lax.axis_index("stream")]
    mine = jnp.where(even, mine, streams - 1 - mine)
    region = lax.dynamic_slice_in_dim(region, mine * rows, rows, 0)[:, None, :, None]
    deriv_zt, filter_zt = deriv_z.T, filter_z.T

    mats = (deriv_x, deriv_zt, filter_x, filter_zt)
    if rows >= 2:
        parts = steps_call(streams, slabs, parts, region[:, 0], *mats)
        return parts.transpose(2, 3, 0, 1, 4).reshape(1, count, width_x, width_y, nz)
    parts = jnp.where(even, jnp.stack([parts[p] for p in place]), jnp.stack([parts[p] for p in back]))
    parts = lax.all_to_all(parts, "stream", split_axis=0, concat_axis=0, tiled=True)
    fields = parts.transpose(1, 2, 0, 3, 4).reshape(rows, count, nx, nz)
    fields = plain_steps(order, fields, region, *mats)

    parts = fields.reshape(rows, count, streams, width_x, nz).transpose(2, 0, 1, 3, 4)
    parts = lax.all_to_all(parts, "stream", split_axis=0, concat_axis=0, tiled=True)
    inv_place = [place.index(j) for j in range(streams)]
    inv_back = [back.index(j) for j in range(streams)]
    parts = jnp.where(even, jnp.stack([parts[p] for p in inv_place]), jnp.stack([parts[p] for p in inv_back]))
    return parts.transpose(2, 3, 0, 1, 4).reshape(1, count, width_x, width_y, nz)


def solution(mesh):
    placed = (P("section", None, "stream", "slab", None), P(None, "slab"), P(), P(), P(), P())
    return jax.shard_map(
        shards,
        mesh=mesh,
        in_specs=placed,
        out_specs=P("section", None, "stream", "slab", None),
        check_vma=False,
    )
```
